32 devices in a mesh: phase: 2 (over core), tok: 4 (over z), mp: 4 (over y, x).
Axes of the slice: x: 2, y: 2, z: 4, core: 2. Of those that a mesh axis runs over, the one named last changes fastest.
Arguments:
- hidden: bfloat16 [2, 512, 6656], P('phase', 'tok', 'mp'), may hold values from -30 to 30
- w_qkv: bfloat16 [2, 6656, 3, 4096], P('phase', 'mp', None, 'tok'), may hold values from -1 to 1
- segment_ids: int32 [2, 512], P('phase'), may hold values from 0 to 3, never falling along the last dimension, each value on 1 to 256 neighbouring positions
- exit_flags: int32 [2, 4], P('phase'), may hold values from 0 to 1, as said below
Outputs:
- attended: bfloat16 [2, 512, 4096], P('phase', 'mp', 'tok')
- handed: bfloat16 [2, 512, 4096], P('phase', 'mp', 'tok')
The draws below stay inside these ranges and needn't reach their ends.
Inputs may be any that keep to these rules, and one draw needn't show every extreme that they name: `exit_flags`: in each micro-batch exactly 2 of the 4 blocks have flag 0.
All inputs are finite; a program needn't handle non-finite values.
Results may differ from the reference program's by a relative error of at most 0.0068.
Values may be sent and summed in bfloat16 or wider, within the bound.
A program may use at most 64 MiB of HBM per device.

```python
import math
import jax
import jax.numpy as jnp
import numpy as np
from jax import lax

D = 6656
HEADS = 32
HEAD = 128
BLOCK = 128
SEGS = 4
TOKENS = 512
BLOCKS = 4
SURV_BLK = 2
N_PHASE = 2


def draw_hidden(key, part):
    first = jax.random.fold_in(key, 11)
    rows = jnp.clip(jax.random.normal(first, (N_PHASE, TOKENS, D), jnp.float32), -6.0, 6.0)
    return rows.astype(jnp.bfloat16)


def draw_w_qkv(key, part):
    first = jax.random.fold_in(key, 21)
    weights = jnp.clip(jax.random.normal(first, (N_PHASE, D, 3, HEADS * HEAD), jnp.float32), -4.0, 4.0) / math.sqrt(D)
    return weights.astype(jnp.bfloat16)


def draw_exit_flags(key, part):
    first = jax.random.fold_in(key, 31)
    phase_keys = jax.random.split(first, N_PHASE)
    ranks = jax.vmap(lambda one: jax.random.permutation(one, BLOCKS))(phase_keys)
    return (ranks >= SURV_BLK).astype(jnp.int32)


def length_profile(count, total, bound, lean):
    portions = [(1 << 20) // math.isqrt(grade ** lean) + 1 for grade in range(2, count + 1)]
    rest, counts = total - bound - (count - 1), [1] * (count - 1)
    while rest > 0:
        candidates = [i for i in range(count - 1) if counts[i] < bound]
        mass, remaining = sum([portions[i] for i in candidates]), rest
        for i in candidates:
            more = min(bound - counts[i], max(1, remaining * portions[i] // mass), rest)
            counts[i] = counts[i] + more
            rest = rest - more
    return np.array([bound] + counts)


def ragged_sizes(key, number_of, total, most, skew):
    if number_of == 2:
        one = jax.random.randint(key, (), max(1, total - most), min(most, total - 1) + 1)
        return jnp.stack([one, total - one])
    tallies = jnp.asarray(length_profile(number_of, total, most, skew), jnp.int32)
    pairs = (number_of - 1) // 2
    giver, taker = tallies[1:1 + 2 * pairs:2], tallies[2:2 + 2 * pairs:2]
    slack = jnp.minimum(giver - 1, most - taker)
    passed = jax.random.randint(jax.random.fold_in(key, 1), (pairs,), 0, 1 << 20) % (slack + 1)
    tallies = tallies.at[1:1 + 2 * pairs:2].set(giver - passed).at[2:2 + 2 * pairs:2].set(taker + passed)
    return tallies[jax.random.permutation(jax.random.fold_in(key, 2), number_of)]


def setup_inputs(seed: int = 0) -> dict:
    key_of = jax.random.split(jax.random.key(seed), 5)
    hidden = draw_hidden(jax.random.fold_in(key_of[4], 71), 0)
    w_qkv = draw_w_qkv(jax.random.fold_in(key_of[4], 71), 0)
    segment_ids = jax.vmap(lambda own: jnp.searchsorted(jnp.cumsum(ragged_sizes(own, SEGS, TOKENS, TOKENS // 2, 0)), jnp.arange(TOKENS), side="right"))(jax.random.split(key_of[2], N_PHASE)).reshape((N_PHASE, TOKENS)).astype(jnp.int32)
    exit_flags = draw_exit_flags(jax.random.fold_in(key_of[4], 71), 0)
    return dict(hidden=hidden, w_qkv=w_qkv, segment_ids=segment_ids, exit_flags=exit_flags)


def attend_head(trio, segment):
    query, keys, values = trio
    total = query.shape[0]
    scores = jnp.dot(query, keys.T, preferred_element_type=jnp.float32) * (1.0 / math.sqrt(HEAD))
    positions = jnp.arange(total, dtype=jnp.int32)
    allowed = (positions[None, :] <= positions[:, None]) & (segment[None, :] == segment[:, None])
    scores = jnp.where(allowed, scores, -1e+30)
    peak = lax.optimization_barrier(jnp.max(scores, axis=-1, keepdims=True))
    expo = jnp.exp(scores - peak)
    probs = (expo / lax.optimization_barrier(jnp.sum(expo, axis=-1, keepdims=True))).astype(jnp.bfloat16)
    return jnp.dot(probs, values, preferred_element_type=jnp.float32)

def reference(hidden, w_qkv, segment_ids, exit_flags):
    results = []
    for phase in range(N_PHASE):
        rows = hidden[phase]
        query = jnp.dot(rows, w_qkv[phase, :, 0, :], preferred_element_type=jnp.float32).astype(jnp.bfloat16)
        keys = jnp.dot(rows, w_qkv[phase, :, 1, :], preferred_element_type=jnp.float32).astype(jnp.bfloat16)
        values = jnp.dot(rows, w_qkv[phase, :, 2, :], preferred_element_type=jnp.float32).astype(jnp.bfloat16)

        def split_heads(matrix):
            return matrix.reshape(TOKENS, HEADS, HEAD).transpose(1, 0, 2)
        segment = segment_ids[phase]
        mixed = lax.map(lambda trio: attend_head(trio, segment), (split_heads(query), split_heads(keys), split_heads(values)))
        mixed = mixed.transpose(1, 0, 2).reshape(TOKENS, HEADS * HEAD)
        alive = jnp.repeat(exit_flags[phase] == 0, BLOCK)
        results.append(jnp.where(alive[:, None], mixed, 0.0).astype(jnp.bfloat16))
    attended = jnp.stack(results)
    handed = jnp.roll(attended, 1, axis=0)
    return (attended, handed)
```

```python
import functools
import math

import jax
import jax.numpy as jnp
from jax import lax
from jax.experimental import pallas as pl
from jax.experimental.pallas import tpu as pltpu
from jax.sharding import PartitionSpec as P

HEAD = 128
BLOCK = 128
CHUNKS = 2
MESH = pl.DeviceIdType.MESH


def remote(src, dst, send, recv, where):
    return pltpu.make_async_remote_copy(
        src_ref=src, dst_ref=dst, send_sem=send, recv_sem=recv, device_id=where, device_id_type=MESH
    )


def fused_kernel(
    tiers, groups, x_ref, w_ref, seg_ref, flag_ref, att_ref, hand_ref,
    hid, wbuf, sendb, recvb, acc, qkv, outb,
    own_sem, w_sem, up_sem, down_sem, gather_sem, rs_send, rs_recv, a_send, a_recv, h_send, h_recv,
):
    p = lax.axis_index("phase")
    z = lax.axis_index("tok")
    m = lax.axis_index("mp")
    rows = x_ref.shape[0]
    piece = rows // CHUNKS
    cols = w_ref.shape[2] // groups
    total = rows * tiers
    quarter = total // groups
    scale = 1.0 / math.sqrt(HEAD)

    def columns(member):
        return pl.ds(pl.multiple_of(member * cols, HEAD), cols)

    own = pltpu.make_async_copy(x_ref, hid.at[z], own_sem)
    own.start()

    def weights(j):
        dest = (m + j) % groups
        return pltpu.make_async_copy(w_ref.at[:, :, columns(dest)], wbuf.at[j], w_sem.at[j])

    for j in [*range(1, groups), 0]:
        weights(j).start()

    barrier = pltpu.get_barrier_semaphore()

    @pl.when(z > 0)
    def _():
        pl.semaphore_signal(barrier, inc=1, device_id={"tok": z - 1}, device_id_type=MESH)

    @pl.when(z < tiers - 1)
    def _():
        pl.semaphore_signal(barrier, inc=1, device_id={"tok": z + 1}, device_id_type=MESH)

    for j in range(1, groups):
        pl.semaphore_signal(
            barrier, inc=1, device_id={"mp": (m + j) % groups}, device_id_type=MESH
        )
    pl.semaphore_signal(barrier, inc=1, device_id={"phase": 1 - p}, device_id_type=MESH)
    pl.semaphore_wait(barrier, groups + jnp.minimum(z, 1) + jnp.minimum(tiers - 1 - z, 1))

    def part(c):
        return pl.ds(c * piece, piece)

    def upward(src, t, c):
        return remote(
            src, hid.at[t, part(c)], up_sem.at[t, c], gather_sem.at[t, c], {"tok": z + 1}
        )

    def downward(src, t, c):
        return remote(
            src, hid.at[t, part(c)], down_sem.at[t, c], gather_sem.at[t, c], {"tok": z - 1}
        )

    for c in range(CHUNKS):

        @pl.when(z < tiers - 1)
        def _():
            upward(x_ref.at[part(c)], z, c).start()

        @pl.when(z > 0)
        def _():
            downward(x_ref.at[part(c)], z, c).start()

    def relay(d):
        for c in range(CHUNKS):

            @pl.when(z - d >= 0)
            def _():
                t = z - d
                src = hid.at[t, part(c)]
                upward(src, t, c).wait_recv()

                @pl.when(z < tiers - 1)
                def _():
                    upward(src, t, c).start()

            @pl.when(z + d < tiers)
            def _():
                t = z + d
                src = hid.at[t, part(c)]
                downward(src, t, c).wait_recv()

                @pl.when(z > 0)
                def _():
                    downward(src, t, c).start()

    near = jnp.minimum(z, tiers - 1 - z)

    def shard_at(s):
        d = (s + 1) // 2
        paired = jnp.where(s % 2 == 1, z - d, z + d)
        far = s - near
        single = jnp.where(z <= tiers - 1 - z, z + far, z - far)
        return jnp.where(s <= 2 * near, paired, single)

    def scatter(j, t):
        return remote(
            sendb.at[j - 1, t], recvb.at[j - 1, t], rs_send.at[j - 1, t], rs_recv.at[j - 1, t],
            {"mp": (m + j) % groups},
        )

    def multiply(s, t):
        @pl.loop(1, groups)
        def _(j):
            @pl.when(s == 0)
            def _():
                weights(j).wait()

            for c in range(3):
                got = jnp.dot(hid[t], wbuf[j, c], preferred_element_type=jnp.float32)
                sendb[j - 1, t, :, c * cols : (c + 1) * cols] = got.astype(jnp.bfloat16)
            scatter(j, t).start()

        @pl.when(s == 0)
        def _():
            weights(0).wait()

        for c in range(3):
            acc[t, :, c * cols : (c + 1) * cols] = jnp.dot(
                hid[t], wbuf[0, c], preferred_element_type=jnp.float32
            )

    def finish(t):
        for j in range(1, groups):
            scatter(j, t).wait_recv()
        for c in range(3):
            span = slice(c * cols, (c + 1) * cols)
            value = acc[t, :, span]
            for j in range(1, groups):
                value = value + recvb[j - 1, t, :, span].astype(jnp.float32)
            qkv[c, pl.ds(pl.multiple_of(t * rows, rows), rows), :] = value.astype(jnp.bfloat16)

    own.wait()

    @pl.loop(0, tiers)
    def _(s):
        @pl.when(s > 0)
        def _():
            relay(s)

        multiply(s, shard_at(s))

        @pl.when(s > 0)
        def _():
            finish(shard_at(s - 1))

    finish(shard_at(tiers - 1))

    def exchange(j):
        return remote(
            outb.at[j - 1], att_ref.at[:, columns(m)], a_send.at[j - 1], a_recv.at[j - 1],
            {"mp": (m + j) % groups},
        )

    def hand(j, member, src):
        return remote(
            src, hand_ref.at[:, columns(member)], h_send.at[j - 1], h_recv.at[j - 1],
            {"phase": 1 - p},
        )

    seg_keys = seg_ref[...]
    key_pos = lax.broadcasted_iota(jnp.int32, (BLOCK, total), 1)
    row_pos = lax.broadcasted_iota(jnp.int32, (BLOCK, total), 0)

    @pl.loop(1, groups + 1)
    def _(j):
        r = (m + j) % groups
        for b in range(quarter // BLOCK):
            first = pl.multiple_of(r * quarter + b * BLOCK, BLOCK)
            here = pl.ds(first, BLOCK)
            seg_rows = jnp.broadcast_to(seg_ref[:, here], (BLOCK, BLOCK)).T
            seg_rows = jnp.concatenate([seg_rows] * (total // BLOCK), axis=1)
            allowed = (key_pos <= row_pos + first) & (seg_rows == seg_keys)
            flag = flag_ref[0, r * (quarter // BLOCK) + b]
            kept = jnp.full((BLOCK, HEAD), flag, jnp.int32) == 0
            for h in range(cols // HEAD):
                head = slice(h * HEAD, (h + 1) * HEAD)
                scores = (
                    lax.dot_general(
                        qkv[0, here, head], qkv[1, :, head], (((1,), (1,)), ((), ())),
                        preferred_element_type=jnp.float32,
                    )
                    * scale
                )
                scores = jnp.where(allowed, scores, -1e30)
                peak = jnp.max(scores, axis=-1, keepdims=True)
                expo = jnp.exp(scores - peak)
                probs = (expo / jnp.sum(expo, axis=-1, keepdims=True)).astype(jnp.bfloat16)
                mixed = jnp.dot(probs, qkv[2, :, head], preferred_element_type=jnp.float32)
                outb[j - 1, b * BLOCK : (b + 1) * BLOCK, head] = jnp.where(
                    kept, mixed, 0.0
                ).astype(jnp.bfloat16)

        @pl.when(j < groups)
        def _():
            exchange(j).start()

    hand(groups, m, outb.at[groups - 1]).start()
    att_ref[:, columns(m)] = outb[groups - 1]
    for j in range(1, groups):
        member = (m + groups - j) % groups
        exchange(j).wait_recv()
        hand(j, member, att_ref.at[:, columns(member)]).start()

    for c in range(CHUNKS):
        for t in range(tiers):

            @pl.when((z >= t) & (z < tiers - 1))
            def _():
                upward(hid.at[t, part(c)], t, c).wait_send()

            @pl.when((z <= t) & (z > 0))
            def _():
                downward(hid.at[t, part(c)], t, c).wait_send()

    for j in range(1, groups):
        for t in range(tiers):
            scatter(j, t).wait_send()
        exchange(j).wait_send()
    for j in range(1, groups + 1):
        hand(j, m, outb.at[groups - 1]).wait()


def local_fused(hidden, w_qkv, segment_ids, exit_flags):
    rows = hidden[0]
    weights = jnp.transpose(w_qkv[0], (1, 0, 2))
    tiers = lax.axis_size("tok")
    groups = lax.axis_size("mp")
    count, width = rows.shape
    head_cols = weights.shape[2]
    cols = head_cols // groups
    total = count * tiers
    quarter = total // groups
    out = jax.ShapeDtypeStruct((quarter, head_cols), jnp.bfloat16)
    dma = pltpu.SemaphoreType.DMA
    attended, handed = pl.pallas_call(
        functools.partial(fused_kernel, tiers, groups),
        out_shape=(out, out),
        in_specs=[
            pl.BlockSpec(memory_space=pl.ANY),
            pl.BlockSpec(memory_space=pl.ANY),
            pl.BlockSpec(memory_space=pltpu.VMEM),
            pl.BlockSpec(memory_space=pltpu.SMEM),
        ],
        out_specs=(pl.BlockSpec(memory_space=pltpu.VMEM),) * 2,
        scratch_shapes=[
            pltpu.VMEM((tiers, count, width), jnp.bfloat16),
            pltpu.VMEM((groups, 3, width, cols), jnp.bfloat16),
            pltpu.VMEM((groups - 1, tiers, count, 3 * cols), jnp.bfloat16),
            pltpu.VMEM((groups - 1, tiers, count, 3 * cols), jnp.bfloat16),
            pltpu.VMEM((tiers, count, 3 * cols), jnp.float32),
            pltpu.VMEM((3, total, cols), jnp.bfloat16),
            pltpu.VMEM((groups, quarter, cols), jnp.bfloat16),
            dma(()),
            dma((groups,)),
            dma((tiers, CHUNKS)),
            dma((tiers, CHUNKS)),
            dma((tiers, CHUNKS)),
            dma((groups - 1, tiers)),
            dma((groups - 1, tiers)),
            dma((groups - 1,)),
            dma((groups - 1,)),
            dma((groups,)),
            dma((groups,)),
        ],
        compiler_params=pltpu.CompilerParams(
            collective_id=0, has_side_effects=True, vmem_limit_bytes=60 * 1024 * 1024
        ),
    )(rows, weights, segment_ids, exit_flags)
    return (attended[None], handed[None])


def shifted(block, axis, distance):
    devices = range(lax.axis_size(axis))
    route = [((i - distance) % len(devices), i) for i in devices]
    return lax.ppermute(block, axis, route)


def attend(query, keys, values, query_pos, segment, key_pos):
    heads_here = query.shape[1] // HEAD
    total = keys.shape[0]
    key_heads = keys.reshape(total, heads_here, HEAD)
    value_heads = values.reshape(total, heads_here, HEAD)
    key_segment = jnp.take(segment, key_pos)
    scale = 1.0 / math.sqrt(HEAD)
    block_rows = query.shape[0]
    scores = (
        jnp.einsum(
            "rhd,shd->hrs",
            query.reshape(block_rows, heads_here, HEAD),
            key_heads,
            preferred_element_type=jnp.float32,
        )
        * scale
    )
    own_segment = jnp.take(segment, query_pos)
    allowed = (key_pos[None, :] <= query_pos[:, None]) & (
        key_segment[None, :] == own_segment[:, None]
    )
    scores = jnp.where(allowed[None], scores, -1e30)
    peak = jnp.max(scores, axis=-1, keepdims=True)
    expo = jnp.exp(scores - peak)
    probs = (expo / jnp.sum(expo, axis=-1, keepdims=True)).astype(jnp.bfloat16)
    mixed = jnp.einsum("hrs,shd->rhd", probs, value_heads, preferred_element_type=jnp.float32)
    return mixed.reshape(block_rows, heads_here * HEAD).astype(jnp.bfloat16)


def local(hidden, w_qkv, segment_ids, exit_flags):
    rows_here = hidden[0]
    weights = w_qkv[0]
    width_here = rows_here.shape[1]
    head_cols = weights.shape[2]
    flat_weights = weights.reshape(width_here, 3 * head_cols)
    segment = segment_ids[0]
    flags = exit_flags[0]
    groups = lax.axis_size("mp")
    member = lax.axis_index("mp")
    partial_value = jnp.dot(
        lax.all_gather(rows_here, "tok", axis=0, tiled=True),
        flat_weights,
        preferred_element_type=jnp.float32,
    )
    total = partial_value.shape[0]
    quarter = total // groups
    query_part = partial_value[:, :head_cols]
    key_value_part = partial_value[:, head_cols:]
    my_pos = member * quarter + jnp.arange(quarter, dtype=jnp.int32)
    my_blocks = my_pos // BLOCK
    alive = jnp.take(flags, my_blocks) == 0
    query = lax.psum_scatter(query_part, "mp", scatter_dimension=0, tiled=True).astype(jnp.bfloat16)
    mine = lax.psum_scatter(key_value_part, "mp", scatter_dimension=0, tiled=True).astype(
        jnp.bfloat16
    )
    key_value = lax.all_gather(mine, "mp", axis=0, tiled=True)
    all_pos = jnp.arange(total, dtype=jnp.int32)
    mixed = attend(
        query, key_value[:, :head_cols], key_value[:, head_cols:], my_pos, segment, all_pos
    )
    zeros = jnp.zeros((quarter, head_cols), jnp.bfloat16)
    result = jnp.where(alive[:, None], mixed, zeros)
    handed = shifted(result, "phase", 1)
    return (result[None], handed[None])


def solution(mesh):
    in_specs = (
        P("phase", "tok", "mp"),
        P("phase", "mp", None, "tok"),
        P("phase", None),
        P("phase", None),
    )
    out_specs = (P("phase", "mp", "tok"), P("phase", "mp", "tok"))
    sizes = dict(mesh.shape)

    def step(hidden, w_qkv, segment_ids, exit_flags):
        heads_here = w_qkv.shape[3] // sizes["tok"] // HEAD
        quarter = hidden.shape[1] // sizes["mp"]
        by_head = heads_here % sizes["mp"] == 0 and quarter % BLOCK == 0 and sizes["phase"] == 2
        body = local_fused if by_head else local
        return jax.shard_map(
            body, mesh=mesh, in_specs=in_specs, out_specs=out_specs, check_vma=False
        )(hidden, w_qkv, segment_ids, exit_flags)

    return step
```

```python
import functools
import math

import jax
import jax.numpy as jnp
from jax import lax
from jax.experimental import pallas as pl
from jax.experimental.pallas import tpu as pltpu
from jax.sharding import PartitionSpec as P

HEAD = 128
BLOCK = 128
CHUNKS = 2
MESH = pl.DeviceIdType.MESH


def remote(src, dst, send, recv, where):
    return pltpu.make_async_remote_copy(
        src_ref=src, dst_ref=dst, send_sem=send, recv_sem=recv, device_id=where, device_id_type=MESH
    )


def fused_kernel(
    tiers, groups, x_ref, w_ref, seg_ref, flag_ref, att_ref, hand_ref,
    hid, wbuf, sendb, recvb, acc, qkv, outb, pend,
    own_sem, w_sem, up_sem, down_sem, gather_sem, rs_send, rs_recv, a_send, a_recv, h_send, h_recv,
):
    p = lax.axis_index("phase")
    z = lax.axis_index("tok")
    m = lax.axis_index("mp")
    rows = x_ref.shape[0]
    piece = rows // CHUNKS
    cols = w_ref.shape[2] // groups
    total = rows * tiers
    quarter = total // groups
    scale = 1.0 / math.sqrt(HEAD)

    half = 3 * cols // 2
    halves = (slice(0, half), slice(half, 3 * cols))

    def peer(j):
        return (m // 2 + j // 2) % 2 * 2 + (m % 2 + j % 2) % 2

    def columns(member):
        return pl.ds(pl.multiple_of(member * cols, HEAD), cols)

    own = pltpu.make_async_copy(x_ref, hid.at[z], own_sem)
    own.start()

    def weights(j):
        dest = peer(j)
        return pltpu.make_async_copy(w_ref.at[:, :, columns(dest)], wbuf.at[j], w_sem.at[j])

    for j in (3, 1, 2, 0):
        weights(j).start()

    barrier = pltpu.get_barrier_semaphore()

    @pl.when(z > 0)
    def _():
        pl.semaphore_signal(barrier, inc=1, device_id={"tok": z - 1}, device_id_type=MESH)

    @pl.when(z < tiers - 1)
    def _():
        pl.semaphore_signal(barrier, inc=1, device_id={"tok": z + 1}, device_id_type=MESH)

    for j in range(1, groups):
        pl.semaphore_signal(
            barrier, inc=1, device_id={"mp": peer(j)}, device_id_type=MESH
        )
    pl.semaphore_signal(barrier, inc=1, device_id={"phase": 1 - p}, device_id_type=MESH)
    pl.semaphore_wait(barrier, groups + jnp.minimum(z, 1) + jnp.minimum(tiers - 1 - z, 1))

    def part(c):
        return pl.ds(pl.multiple_of(c * piece, piece), piece)

    def upward(src, t, c):
        return remote(
            src, hid.at[t, part(c)], up_sem.at[t, c], gather_sem.at[t, c], {"tok": z + 1}
        )

    def downward(src, t, c):
        return remote(
            src, hid.at[t, part(c)], down_sem.at[t, c], gather_sem.at[t, c], {"tok": z - 1}
        )

    for c in range(CHUNKS):

        @pl.when(z < tiers - 1)
        def _():
            upward(x_ref.at[part(c)], z, c).start()

        @pl.when(z > 0)
        def _():
            downward(x_ref.at[part(c)], z, c).start()

    def relay(d, c):
        @pl.when(z - d >= 0)
        def _():
            t = z - d
            src = hid.at[t, part(c)]
            upward(src, t, c).wait_recv()

            @pl.when(z < tiers - 1)
            def _():
                upward(src, t, c).start()

        @pl.when(z + d < tiers)
        def _():
            t = z + d
            src = hid.at[t, part(c)]
            downward(src, t, c).wait_recv()

            @pl.when(z > 0)
            def _():
                downward(src, t, c).start()

    near = jnp.minimum(z, tiers - 1 - z)

    def shard_at(s):
        d = (s + 1) // 2
        paired = jnp.where(s % 2 == 1, z - d, z + d)
        far = s - near
        single = jnp.where(z <= tiers - 1 - z, z + far, z - far)
        return jnp.where(s <= 2 * near, paired, single)

    def scatter(j, t, c, h):
        where = peer(j) if j < 3 else peer(2 - h)
        return remote(
            sendb.at[j - 1, t, part(c), halves[h]], recvb.at[j - 1, t, part(c), halves[h]],
            rs_send.at[j - 1, t, c, h], rs_recv.at[j - 1, t, c, h], {"mp": where},
        )

    def product(n, t, c, j):
        @pl.when(n == 0)
        def _():
            weights(j).wait()

        return [
            jnp.dot(hid[t, part(c), :], wbuf[j, k], preferred_element_type=jnp.float32)
            for k in range(3)
        ]

    def multiply(n, t, c):
        got = jnp.concatenate(product(n, t, c, 3), axis=1)
        sendb[2, t, part(c), :] = got.astype(jnp.bfloat16)
        scatter(3, t, c, 0).start()
        scatter(3, t, c, 1).start()
        for j in (1, 2):
            held, direct = halves[j - 1], halves[2 - j]
            got = jnp.concatenate(product(n, t, c, j), axis=1)
            sendb[j - 1, t, part(c), direct] = got[:, direct].astype(jnp.bfloat16)
            scatter(j, t, c, 2 - j).start()
            pend[t, part(c), held] = got[:, held]
        acc[t, part(c), :] = jnp.concatenate(product(n, t, c, 0), axis=1)

    def combine(t, c):
        for j in (1, 2):
            held = halves[j - 1]
            scatter(3, t, c, j - 1).wait_recv()
            total_here = pend[t, part(c), held] + recvb[2, t, part(c), held].astype(jnp.float32)
            sendb[j - 1, t, part(c), held] = total_here.astype(jnp.bfloat16)
            scatter(j, t, c, j - 1).start()

    def finish(t, c):
        for j in (1, 2):
            for h in range(2):
                scatter(j, t, c, h).wait_recv()
        first = pl.multiple_of(t * rows + c * piece, piece)
        for k in range(3):
            span = slice(k * cols, (k + 1) * cols)
            value = acc[t, part(c), span]
            for j in (1, 2):
                value = value + recvb[j - 1, t, part(c), span].astype(jnp.float32)
            qkv[k, pl.ds(first, piece), :] = value.astype(jnp.bfloat16)

    steps = tiers * CHUNKS

    def at(n):
        return shard_at(n // CHUNKS), n % CHUNKS

    own.wait()

    @pl.loop(0, steps)
    def _(n):
        @pl.when(n >= CHUNKS)
        def _():
            relay(n // CHUNKS, n % CHUNKS)

        multiply(n, *at(n))

        @pl.when(n > 0)
        def _():
            combine(*at(n - 1))

        @pl.when(n > 1)
        def _():
            finish(*at(n - 2))

    combine(*at(steps - 1))
    finish(*at(steps - 2))
    finish(*at(steps - 1))

    def exchange(j):
        return remote(
            outb.at[j - 1], att_ref.at[:, columns(m)], a_send.at[j - 1], a_recv.at[j - 1],
            {"mp": peer(j)},
        )

    def hand(j, member, src):
        return remote(
            src, hand_ref.at[:, columns(member)], h_send.at[j - 1], h_recv.at[j - 1],
            {"phase": 1 - p},
        )

    seg_keys = seg_ref[...]
    key_pos = lax.broadcasted_iota(jnp.int32, (BLOCK, total), 1)
    row_pos = lax.broadcasted_iota(jnp.int32, (BLOCK, total), 0)

    @pl.loop(1, groups + 1)
    def _(j):
        r = peer(j)
        for b in range(quarter // BLOCK):
            first = pl.multiple_of(r * quarter + b * BLOCK, BLOCK)
            here = pl.ds(first, BLOCK)
            seg_rows = jnp.broadcast_to(seg_ref[:, here], (BLOCK, BLOCK)).T
            seg_rows = jnp.concatenate([seg_rows] * (total // BLOCK), axis=1)
            allowed = (key_pos <= row_pos + first) & (seg_rows == seg_keys)
            flag = flag_ref[0, r * (quarter // BLOCK) + b]
            kept = jnp.full((BLOCK, HEAD), flag, jnp.int32) == 0
            for h in range(cols // HEAD):
                head = slice(h * HEAD, (h + 1) * HEAD)
                scores = (
                    lax.dot_general(
                        qkv[0, here, head], qkv[1, :, head], (((1,), (1,)), ((), ())),
                        preferred_element_type=jnp.float32,
                    )
                    * scale
                )
                scores = jnp.where(allowed, scores, -1e30)
                peak = jnp.max(scores, axis=-1, keepdims=True)
                expo = jnp.exp(scores - peak)
                probs = (expo / jnp.sum(expo, axis=-1, keepdims=True)).astype(jnp.bfloat16)
                mixed = jnp.dot(probs, qkv[2, :, head], preferred_element_type=jnp.float32)
                outb[j - 1, b * BLOCK : (b + 1) * BLOCK, head] = jnp.where(
                    kept, mixed, 0.0
                ).astype(jnp.bfloat16)

        @pl.when(j < groups)
        def _():
            exchange(j).start()

    hand(groups, m, outb.at[groups - 1]).start()
    att_ref[:, columns(m)] = outb[groups - 1]
    for j in range(1, groups):
        member = peer(j)
        exchange(j).wait_recv()
        hand(j, member, att_ref.at[:, columns(member)]).start()

    for c in range(CHUNKS):
        for t in range(tiers):

            @pl.when((z >= t) & (z < tiers - 1))
            def _():
                upward(hid.at[t, part(c)], t, c).wait_send()

            @pl.when((z <= t) & (z > 0))
            def _():
                downward(hid.at[t, part(c)], t, c).wait_send()

    for j in range(1, groups):
        for t in range(tiers):
            for c in range(CHUNKS):
                for h in range(2):
                    scatter(j, t, c, h).wait_send()
        exchange(j).wait_send()
    for j in range(1, groups + 1):
        hand(j, m, outb.at[groups - 1]).wait()


def local_fused(hidden, w_qkv, segment_ids, exit_flags):
    rows = hidden[0]
    weights = jnp.transpose(w_qkv[0], (1, 0, 2))
    tiers = lax.axis_size("tok")
    groups = lax.axis_size("mp")
    count, width = rows.shape
    head_cols = weights.shape[2]
    cols = head_cols // groups
    total = count * tiers
    quarter = total // groups
    out = jax.ShapeDtypeStruct((quarter, head_cols), jnp.bfloat16)
    dma = pltpu.SemaphoreType.DMA
    attended, handed = pl.pallas_call(
        functools.partial(fused_kernel, tiers, groups),
        out_shape=(out, out),
        in_specs=[
            pl.BlockSpec(memory_space=pl.ANY),
            pl.BlockSpec(memory_space=pl.ANY),
            pl.BlockSpec(memory_space=pltpu.VMEM),
            pl.BlockSpec(memory_space=pltpu.SMEM),
        ],
        out_specs=(pl.BlockSpec(memory_space=pltpu.VMEM),) * 2,
        scratch_shapes=[
            pltpu.VMEM((tiers, count, width), jnp.bfloat16),
            pltpu.VMEM((groups, 3, width, cols), jnp.bfloat16),
            pltpu.VMEM((groups - 1, tiers, count, 3 * cols), jnp.bfloat16),
            pltpu.VMEM((groups - 1, tiers, count, 3 * cols), jnp.bfloat16),
            pltpu.VMEM((tiers, count, 3 * cols), jnp.float32),
            pltpu.VMEM((3, total, cols), jnp.bfloat16),
            pltpu.VMEM((groups, quarter, cols), jnp.bfloat16),
            pltpu.VMEM((tiers, count, 3 * cols), jnp.float32),
            dma(()),
            dma((groups,)),
            dma((tiers, CHUNKS)),
            dma((tiers, CHUNKS)),
            dma((tiers, CHUNKS)),
            dma((groups - 1, tiers, CHUNKS, 2)),
            dma((groups - 1, tiers, CHUNKS, 2)),
            dma((groups - 1,)),
            dma((groups - 1,)),
            dma((groups,)),
            dma((groups,)),
        ],
        compiler_params=pltpu.CompilerParams(
            collective_id=0, has_side_effects=True, vmem_limit_bytes=60 * 1024 * 1024
        ),
    )(rows, weights, segment_ids, exit_flags)
    return (attended[None], handed[None])


def shifted(block, axis, distance):
    devices = range(lax.axis_size(axis))
    route = [((i - distance) % len(devices), i) for i in devices]
    return lax.ppermute(block, axis, route)


def attend(query, keys, values, query_pos, segment, key_pos):
    heads_here = query.shape[1] // HEAD
    total = keys.shape[0]
    key_heads = keys.reshape(total, heads_here, HEAD)
    value_heads = values.reshape(total, heads_here, HEAD)
    key_segment = jnp.take(segment, key_pos)
    scale = 1.0 / math.sqrt(HEAD)
    block_rows = query.shape[0]
    scores = (
        jnp.einsum(
            "rhd,shd->hrs",
            query.reshape(block_rows, heads_here, HEAD),
            key_heads,
            preferred_element_type=jnp.float32,
        )
        * scale
    )
    own_segment = jnp.take(segment, query_pos)
    allowed = (key_pos[None, :] <= query_pos[:, None]) & (
        key_segment[None, :] == own_segment[:, None]
    )
    scores = jnp.where(allowed[None], scores, -1e30)
    peak = jnp.max(scores, axis=-1, keepdims=True)
    expo = jnp.exp(scores - peak)
    probs = (expo / jnp.sum(expo, axis=-1, keepdims=True)).astype(jnp.bfloat16)
    mixed = jnp.einsum("hrs,shd->rhd", probs, value_heads, preferred_element_type=jnp.float32)
    return mixed.reshape(block_rows, heads_here * HEAD).astype(jnp.bfloat16)


def local(hidden, w_qkv, segment_ids, exit_flags):
    rows_here = hidden[0]
    weights = w_qkv[0]
    width_here = rows_here.shape[1]
    head_cols = weights.shape[2]
    flat_weights = weights.reshape(width_here, 3 * head_cols)
    segment = segment_ids[0]
    flags = exit_flags[0]
    groups = lax.axis_size("mp")
    member = lax.axis_index("mp")
    partial_value = jnp.dot(
        lax.all_gather(rows_here, "tok", axis=0, tiled=True),
        flat_weights,
        preferred_element_type=jnp.float32,
    )
    total = partial_value.shape[0]
    quarter = total // groups
    query_part = partial_value[:, :head_cols]
    key_value_part = partial_value[:, head_cols:]
    my_pos = member * quarter + jnp.arange(quarter, dtype=jnp.int32)
    my_blocks = my_pos // BLOCK
    alive = jnp.take(flags, my_blocks) == 0
    query = lax.psum_scatter(query_part, "mp", scatter_dimension=0, tiled=True).astype(jnp.bfloat16)
    mine = lax.psum_scatter(key_value_part, "mp", scatter_dimension=0, tiled=True).astype(
        jnp.bfloat16
    )
    key_value = lax.all_gather(mine, "mp", axis=0, tiled=True)
    all_pos = jnp.arange(total, dtype=jnp.int32)
    mixed = attend(
        query, key_value[:, :head_cols], key_value[:, head_cols:], my_pos, segment, all_pos
    )
    zeros = jnp.zeros((quarter, head_cols), jnp.bfloat16)
    result = jnp.where(alive[:, None], mixed, zeros)
    handed = shifted(result, "phase", 1)
    return (result[None], handed[None])


def solution(mesh):
    in_specs = (
        P("phase", "tok", "mp"),
        P("phase", "mp", None, "tok"),
        P("phase", None),
        P("phase", None),
    )
    out_specs = (P("phase", "mp", "tok"), P("phase", "mp", "tok"))
    sizes = dict(mesh.shape)

    def step(hidden, w_qkv, segment_ids, exit_flags):
        heads_here = w_qkv.shape[3] // sizes["tok"] // HEAD
        quarter = hidden.shape[1] // sizes["mp"]
        by_head = heads_here % sizes["mp"] == 0 and quarter % BLOCK == 0 and sizes["phase"] == 2
        by_head = by_head and sizes["mp"] == 4
        body = local_fused if by_head else local
        return jax.shard_map(
            body, mesh=mesh, in_specs=in_specs, out_specs=out_specs, check_vma=False
        )(hidden, w_qkv, segment_ids, exit_flags)

    return step
```

```python
import functools
import math

import jax
import jax.numpy as jnp
from jax import lax
from jax.experimental import pallas as pl
from jax.experimental.pallas import tpu as pltpu
from jax.sharding import PartitionSpec as P

HEAD = 128
BLOCK = 128
CHUNKS = 2
MESH = pl.DeviceIdType.MESH


def remote(src, dst, send, recv, where):
    return pltpu.make_async_remote_copy(
        src_ref=src, dst_ref=dst, send_sem=send, recv_sem=recv, device_id=where, device_id_type=MESH
    )


def fused_kernel(
    tiers, groups, x_ref, w_ref, seg_ref, flag_ref, att_ref, hand_ref,
    hid, wbuf, sendb, recvb, acc, qkv, outb,
    own_sem, w_sem, up_sem, down_sem, gather_sem, rs_send, rs_recv, a_send, a_recv, h_send, h_recv,
):
    p = lax.axis_index("phase")
    z = lax.axis_index("tok")
    m = lax.axis_index("mp")
    rows = x_ref.shape[0]
    piece = rows // CHUNKS
    cols = w_ref.shape[2] // groups
    total = rows * tiers
    quarter = total // groups
    scale = 1.0 / math.sqrt(HEAD)

    def columns(member):
        return pl.ds(pl.multiple_of(member * cols, HEAD), cols)

    own = pltpu.make_async_copy(x_ref, hid.at[z], own_sem)
    own.start()

    def weights(j):
        dest = (m + j) % groups
        return pltpu.make_async_copy(w_ref.at[:, :, columns(dest)], wbuf.at[j], w_sem.at[j])

    for j in [*range(1, groups), 0]:
        weights(j).start()

    barrier = pltpu.get_barrier_semaphore()

    @pl.when(z > 0)
    def _():
        pl.semaphore_signal(barrier, inc=1, device_id={"tok": z - 1}, device_id_type=MESH)

    @pl.when(z < tiers - 1)
    def _():
        pl.semaphore_signal(barrier, inc=1, device_id={"tok": z + 1}, device_id_type=MESH)

    for j in range(1, groups):
        pl.semaphore_signal(
            barrier, inc=1, device_id={"mp": (m + j) % groups}, device_id_type=MESH
        )
    pl.semaphore_signal(barrier, inc=1, device_id={"phase": 1 - p}, device_id_type=MESH)
    pl.semaphore_wait(barrier, groups + jnp.minimum(z, 1) + jnp.minimum(tiers - 1 - z, 1))

    def part(c):
        return pl.ds(pl.multiple_of(c * piece, piece), piece)

    def upward(src, t, c):
        return remote(
            src, hid.at[t, part(c)], up_sem.at[t, c], gather_sem.at[t, c], {"tok": z + 1}
        )

    def downward(src, t, c):
        return remote(
            src, hid.at[t, part(c)], down_sem.at[t, c], gather_sem.at[t, c], {"tok": z - 1}
        )

    for c in range(CHUNKS):

        @pl.when(z < tiers - 1)
        def _():
            upward(x_ref.at[part(c)], z, c).start()

        @pl.when(z > 0)
        def _():
            downward(x_ref.at[part(c)], z, c).start()

    def relay(d, c):
        @pl.when(z - d >= 0)
        def _():
            t = z - d
            src = hid.at[t, part(c)]
            upward(src, t, c).wait_recv()

            @pl.when(z < tiers - 1)
            def _():
                upward(src, t, c).start()

        @pl.when(z + d < tiers)
        def _():
            t = z + d
            src = hid.at[t, part(c)]
            downward(src, t, c).wait_recv()

            @pl.when(z > 0)
            def _():
                downward(src, t, c).start()

    near = jnp.minimum(z, tiers - 1 - z)

    def shard_at(s):
        d = (s + 1) // 2
        paired = jnp.where(s % 2 == 1, z - d, z + d)
        far = s - near
        single = jnp.where(z <= tiers - 1 - z, z + far, z - far)
        return jnp.where(s <= 2 * near, paired, single)

    def scatter(j, t, c):
        return remote(
            sendb.at[j - 1, t, part(c)], recvb.at[j - 1, t, part(c)],
            rs_send.at[j - 1, t, c], rs_recv.at[j - 1, t, c],
            {"mp": (m + j) % groups},
        )

    def multiply(n, t, c):
        @pl.loop(1, groups)
        def _(j):
            @pl.when(n == 0)
            def _():
                weights(j).wait()

            for k in range(3):
                got = jnp.dot(
                    hid[t, part(c), :], wbuf[j, k], preferred_element_type=jnp.float32
                )
                sendb[j - 1, t, part(c), k * cols : (k + 1) * cols] = got.astype(jnp.bfloat16)
            scatter(j, t, c).start()

        @pl.when(n == 0)
        def _():
            weights(0).wait()

        for k in range(3):
            acc[t, part(c), k * cols : (k + 1) * cols] = jnp.dot(
                hid[t, part(c), :], wbuf[0, k], preferred_element_type=jnp.float32
            )

    def finish(t, c):
        for j in range(1, groups):
            scatter(j, t, c).wait_recv()
        for k in range(3):
            span = slice(k * cols, (k + 1) * cols)
            value = acc[t, part(c), span]
            for j in range(1, groups):
                value = value + recvb[j - 1, t, part(c), span].astype(jnp.float32)
            first = pl.multiple_of(t * rows + c * piece, piece)
            qkv[k, pl.ds(first, piece), :] = value.astype(jnp.bfloat16)

    own.wait()

    @pl.loop(0, tiers * CHUNKS)
    def _(n):
        s, c = n // CHUNKS, n % CHUNKS

        @pl.when(s > 0)
        def _():
            relay(s, c)

        multiply(n, shard_at(s), c)

        @pl.when(n > 0)
        def _():
            finish(shard_at((n - 1) // CHUNKS), (n - 1) % CHUNKS)

    finish(shard_at(tiers - 1), CHUNKS - 1)

    def exchange(j):
        return remote(
            outb.at[j - 1], att_ref.at[:, columns(m)], a_send.at[j - 1], a_recv.at[j - 1],
            {"mp": (m + j) % groups},
        )

    def hand(j, member, src):
        return remote(
            src, hand_ref.at[:, columns(member)], h_send.at[j - 1], h_recv.at[j - 1],
            {"phase": 1 - p},
        )

    seg_keys = seg_ref[...]
    key_pos = lax.broadcasted_iota(jnp.int32, (BLOCK, total), 1)
    row_pos = lax.broadcasted_iota(jnp.int32, (BLOCK, total), 0)

    @pl.loop(1, groups + 1)
    def _(j):
        r = (m + j) % groups
        for b in range(quarter // BLOCK):
            first = pl.multiple_of(r * quarter + b * BLOCK, BLOCK)
            here = pl.ds(first, BLOCK)
            seg_rows = jnp.broadcast_to(seg_ref[:, here], (BLOCK, BLOCK)).T
            seg_rows = jnp.concatenate([seg_rows] * (total // BLOCK), axis=1)
            allowed = (key_pos <= row_pos + first) & (seg_rows == seg_keys)
            flag = flag_ref[0, r * (quarter // BLOCK) + b]
            kept = jnp.full((BLOCK, HEAD), flag, jnp.int32) == 0
            for h in range(cols // HEAD):
                head = slice(h * HEAD, (h + 1) * HEAD)
                scores = (
                    lax.dot_general(
                        qkv[0, here, head], qkv[1, :, head], (((1,), (1,)), ((), ())),
                        preferred_element_type=jnp.float32,
                    )
                    * scale
                )
                scores = jnp.where(allowed, scores, -1e30)
                peak = jnp.max(scores, axis=-1, keepdims=True)
                expo = jnp.exp(scores - peak)
                probs = (expo / jnp.sum(expo, axis=-1, keepdims=True)).astype(jnp.bfloat16)
                mixed = jnp.dot(probs, qkv[2, :, head], preferred_element_type=jnp.float32)
                outb[j - 1, b * BLOCK : (b + 1) * BLOCK, head] = jnp.where(
                    kept, mixed, 0.0
                ).astype(jnp.bfloat16)

        @pl.when(j < groups)
        def _():
            exchange(j).start()

    hand(groups, m, outb.at[groups - 1]).start()
    att_ref[:, columns(m)] = outb[groups - 1]
    for j in range(1, groups):
        member = (m + groups - j) % groups
        exchange(j).wait_recv()
        hand(j, member, att_ref.at[:, columns(member)]).start()

    for c in range(CHUNKS):
        for t in range(tiers):

            @pl.when((z >= t) & (z < tiers - 1))
            def _():
                upward(hid.at[t, part(c)], t, c).wait_send()

            @pl.when((z <= t) & (z > 0))
            def _():
                downward(hid.at[t, part(c)], t, c).wait_send()

    for j in range(1, groups):
        for t in range(tiers):
            for c in range(CHUNKS):
                scatter(j, t, c).wait_send()
        exchange(j).wait_send()
    for j in range(1, groups + 1):
        hand(j, m, outb.at[groups - 1]).wait()


def local_fused(hidden, w_qkv, segment_ids, exit_flags):
    rows = hidden[0]
    weights = jnp.transpose(w_qkv[0], (1, 0, 2))
    tiers = lax.axis_size("tok")
    groups = lax.axis_size("mp")
    count, width = rows.shape
    head_cols = weights.shape[2]
    cols = head_cols // groups
    total = count * tiers
    quarter = total // groups
    out = jax.ShapeDtypeStruct((quarter, head_cols), jnp.bfloat16)
    dma = pltpu.SemaphoreType.DMA
    attended, handed = pl.pallas_call(
        functools.partial(fused_kernel, tiers, groups),
        out_shape=(out, out),
        in_specs=[
            pl.BlockSpec(memory_space=pl.ANY),
            pl.BlockSpec(memory_space=pl.ANY),
            pl.BlockSpec(memory_space=pltpu.VMEM),
            pl.BlockSpec(memory_space=pltpu.SMEM),
        ],
        out_specs=(pl.BlockSpec(memory_space=pltpu.VMEM),) * 2,
        scratch_shapes=[
            pltpu.VMEM((tiers, count, width), jnp.bfloat16),
            pltpu.VMEM((groups, 3, width, cols), jnp.bfloat16),
            pltpu.VMEM((groups - 1, tiers, count, 3 * cols), jnp.bfloat16),
            pltpu.VMEM((groups - 1, tiers, count, 3 * cols), jnp.bfloat16),
            pltpu.VMEM((tiers, count, 3 * cols), jnp.float32),
            pltpu.VMEM((3, total, cols), jnp.bfloat16),
            pltpu.VMEM((groups, quarter, cols), jnp.bfloat16),
            dma(()),
            dma((groups,)),
            dma((tiers, CHUNKS)),
            dma((tiers, CHUNKS)),
            dma((tiers, CHUNKS)),
            dma((groups - 1, tiers, CHUNKS)),
            dma((groups - 1, tiers, CHUNKS)),
            dma((groups - 1,)),
            dma((groups - 1,)),
            dma((groups,)),
            dma((groups,)),
        ],
        compiler_params=pltpu.CompilerParams(
            collective_id=0, has_side_effects=True, vmem_limit_bytes=51 * 1024 * 1024
        ),
    )(rows, weights, segment_ids, exit_flags)
    return (attended[None], handed[None])


def shifted(block, axis, distance):
    devices = range(lax.axis_size(axis))
    route = [((i - distance) % len(devices), i) for i in devices]
    return lax.ppermute(block, axis, route)


def attend(query, keys, values, query_pos, segment, key_pos):
    heads_here = query.shape[1] // HEAD
    total = keys.shape[0]
    key_heads = keys.reshape(total, heads_here, HEAD)
    value_heads = values.reshape(total, heads_here, HEAD)
    key_segment = jnp.take(segment, key_pos)
    scale = 1.0 / math.sqrt(HEAD)
    block_rows = query.shape[0]
    scores = (
        jnp.einsum(
            "rhd,shd->hrs",
            query.reshape(block_rows, heads_here, HEAD),
            key_heads,
            preferred_element_type=jnp.float32,
        )
        * scale
    )
    own_segment = jnp.take(segment, query_pos)
    allowed = (key_pos[None, :] <= query_pos[:, None]) & (
        key_segment[None, :] == own_segment[:, None]
    )
    scores = jnp.where(allowed[None], scores, -1e30)
    peak = jnp.max(scores, axis=-1, keepdims=True)
    expo = jnp.exp(scores - peak)
    probs = (expo / jnp.sum(expo, axis=-1, keepdims=True)).astype(jnp.bfloat16)
    mixed = jnp.einsum("hrs,shd->rhd", probs, value_heads, preferred_element_type=jnp.float32)
    return mixed.reshape(block_rows, heads_here * HEAD).astype(jnp.bfloat16)


def local(hidden, w_qkv, segment_ids, exit_flags):
    rows_here = hidden[0]
    weights = w_qkv[0]
    width_here = rows_here.shape[1]
    head_cols = weights.shape[2]
    flat_weights = weights.reshape(width_here, 3 * head_cols)
    segment = segment_ids[0]
    flags = exit_flags[0]
    groups = lax.axis_size("mp")
    member = lax.axis_index("mp")
    partial_value = jnp.dot(
        lax.all_gather(rows_here, "tok", axis=0, tiled=True),
        flat_weights,
        preferred_element_type=jnp.float32,
    )
    total = partial_value.shape[0]
    quarter = total // groups
    query_part = partial_value[:, :head_cols]
    key_value_part = partial_value[:, head_cols:]
    my_pos = member * quarter + jnp.arange(quarter, dtype=jnp.int32)
    my_blocks = my_pos // BLOCK
    alive = jnp.take(flags, my_blocks) == 0
    query = lax.psum_scatter(query_part, "mp", scatter_dimension=0, tiled=True).astype(jnp.bfloat16)
    mine = lax.psum_scatter(key_value_part, "mp", scatter_dimension=0, tiled=True).astype(
        jnp.bfloat16
    )
    key_value = lax.all_gather(mine, "mp", axis=0, tiled=True)
    all_pos = jnp.arange(total, dtype=jnp.int32)
    mixed = attend(
        query, key_value[:, :head_cols], key_value[:, head_cols:], my_pos, segment, all_pos
    )
    zeros = jnp.zeros((quarter, head_cols), jnp.bfloat16)
    result = jnp.where(alive[:, None], mixed, zeros)
    handed = shifted(result, "phase", 1)
    return (result[None], handed[None])


def solution(mesh):
    in_specs = (
        P("phase", "tok", "mp"),
        P("phase", "mp", None, "tok"),
        P("phase", None),
        P("phase", None),
    )
    out_specs = (P("phase", "mp", "tok"), P("phase", "mp", "tok"))
    sizes = dict(mesh.shape)

    def step(hidden, w_qkv, segment_ids, exit_flags):
        heads_here = w_qkv.shape[3] // sizes["tok"] // HEAD
        quarter = hidden.shape[1] // sizes["mp"]
        by_head = heads_here % sizes["mp"] == 0 and quarter % BLOCK == 0 and sizes["phase"] == 2
        body = local_fused if by_head else local
        return jax.shard_map(
            body, mesh=mesh, in_specs=in_specs, out_specs=out_specs, check_vma=False
        )(hidden, w_qkv, segment_ids, exit_flags)

    return step
```
